32 devices in a mesh: gx: 4 (over y, x), gy: 2 (over core), gz: 4 (over z).
Axes of the slice: x: 2, y: 2, z: 4, core: 2. Of those that a mesh axis runs over, the one named last changes fastest.
Arguments:
- frac: float32 [3, 4, 2, 8, 128], P(None, 'gx', 'gy', 'gz'), may hold values from 0 to 1
- velocity: float32 [3, 4, 2, 8, 128], P(None, 'gx', 'gy', 'gz'), may hold values from -2 to 2
- force_old: float32 [3, 4, 2, 8, 128], P(None, 'gx', 'gy', 'gz'), may hold values from -6 to 6
- species: int32 [4, 2, 8, 128], P('gx', 'gy', 'gz'), may hold values from 0 to 9
- cell_count: int32 [4, 2, 8], P('gx', 'gy', 'gz'), may hold values from 1 to 128, as said below
- neighbours: int32 [16, 4, 2, 8, 128], P(None, 'gx', 'gy', 'gz'), may hold values from 0 to 3455, as said below
- embed: bfloat16 [10, 64], replicated, may hold values from -6 to 6
- w_radial_in: bfloat16 [8, 64], replicated, may hold values from -2 to 2
- w_radial_out: bfloat16 [64, 192], replicated, may hold values from -0.75 to 0.75
- w_node: bfloat16 [256, 64], replicated, may hold values from -0.375 to 0.375
- w_energy: float32 [64], replicated, may hold values from -0.75 to 0.75
Outputs:
- next_frac: float32 [3, 4, 2, 8, 128], P(None, 'gx', 'gy', 'gz')
- next_velocity: float32 [3, 4, 2, 8, 128], P(None, 'gx', 'gy', 'gz')
- next_force: float32 [3, 4, 2, 8, 128], P(None, 'gx', 'gy', 'gz')
- site_energy: float32 [4, 2, 8, 128], P('gx', 'gy', 'gz')
The draws below stay inside these ranges and needn't reach their ends.
Inputs may be any that keep to these rules, and one draw needn't show every extreme that they name: `cell_count`: in every draw at least one cell holds exactly 128 atoms; the other cells hold 1 to 128. `neighbours`: each code o * 128 + s names slot s of the cell at offset (o // 9 - 1, (o // 3) % 3 - 1, o % 3 - 1) from the receiver's cell, periodic; s is below that cell's count; no code names the receiver itself.
All inputs are finite; a program needn't handle non-finite values.
Results may differ from the reference program's by a relative error of at most 0.015.
Values may be sent and summed in bfloat16 or wider, within the bound.
A program may use at most 64 MiB of HBM per device.

```python
import math
import jax
import jax.numpy as jnp
import numpy as np
from jax import lax

CH = 64
NB = 8
NSPEC = 10
K = 16
CAP = 128
NX = 4
NY = 2
NZ = 8


def count_field(key):
    key_a, key_b, key_c, key_d = jax.random.split(key, 4)
    first = jax.random.randint(key_a, (NX, NY, NZ), 1, CAP + 1)
    second = jax.random.randint(key_b, (NX, NY, NZ), 1, CAP + 1)
    base = 1 + first * second // CAP
    centre = jax.random.randint(key_c, (3,), 0, 1 << 20)
    grid_a = jnp.arange(NX, dtype=jnp.int32)[:, None, None]
    grid_b = jnp.arange(NY, dtype=jnp.int32)[None, :, None]
    grid_c = jnp.arange(NZ, dtype=jnp.int32)[None, None, :]
    dist_a = (grid_a - centre[0] % NX) % NX
    dist_b = (grid_b - centre[1] % NY) % NY
    dist_c = (grid_c - centre[2] % NZ) % NZ
    inside_a = jnp.minimum(dist_a, NX - dist_a) < max(NX // 4, 1)
    inside_b = jnp.minimum(dist_b, NY - dist_b) < max(NY // 4, 1)
    inside_c = jnp.minimum(dist_c, NZ - dist_c) < max(NZ // 4, 1)
    dense = inside_a & inside_b & inside_c
    counts = jnp.minimum(jnp.where(dense, 3 * base, base), CAP)
    chosen = jax.random.randint(key_d, (), 0, NX * NY * NZ)
    counts = counts.reshape(-1).at[chosen].set(CAP).reshape(NX, NY, NZ)
    return counts.astype(jnp.int32)


def draw_cell_count(key, part):
    return count_field(jax.random.fold_in(key, 7))


def draw_neighbours(key, part):
    counts = count_field(jax.random.fold_in(key, 7))
    key_a, key_b, key_c = jax.random.split(jax.random.fold_in(key, 8), 3)
    shape = (K, NX, NY, NZ, CAP)
    nearby = jax.random.randint(key_a, shape, 0, 2)
    spread = jax.random.randint(key_b, shape, 0, 27)
    offset = jnp.where(nearby == 0, 13, spread)
    grid_a = jnp.arange(NX, dtype=jnp.int32)[None, :, None, None, None]
    grid_b = jnp.arange(NY, dtype=jnp.int32)[None, None, :, None, None]
    grid_c = jnp.arange(NZ, dtype=jnp.int32)[None, None, None, :, None]
    slot_grid = jnp.arange(CAP, dtype=jnp.int32)[None, None, None, None, :]
    target = counts[(grid_a + offset // 9 - 1) % NX, (grid_b + offset // 3 % 3 - 1) % NY, (grid_c + offset % 3 - 1) % NZ]
    picked = jax.random.randint(key_c, shape, 0, 65536)
    slot_id = picked * target // 65536
    itself = (offset == 13) & (slot_id == slot_grid)
    offset = jnp.where(itself, 14, offset)
    slot_id = jnp.where(itself, 0, slot_id)
    return (offset * CAP + slot_id).astype(jnp.int32)


def set_ends(values, own_key, smallest, high):
    longest = values.shape.index(max(values.shape))
    spots = []
    for shift in (0, 1):
        where = [jax.random.randint(jax.random.fold_in(own_key, axis), (), 0, length) for axis, length in enumerate(values.shape)]
        where[longest] = (where[longest] + shift) % values.shape[longest]
        spots.append(tuple(where))
    return values.at[spots[0]].set(smallest).at[spots[1]].set(high)


def block_levels(key, shape, pieces, least, top_value):
    def one(axis_at, parts):
        heights = jax.random.uniform(jax.random.fold_in(jax.random.fold_in(key, 6), axis_at), (parts,), jnp.float32, least / len(pieces), top_value / len(pieces))
        return jnp.repeat(jnp.exp(heights), shape[axis_at] // parts).reshape((-1,) + (1,) * (len(shape) - axis_at - 1))

    loudness = one(*pieces[0])
    for cut in pieces[1:]:
        loudness = loudness * one(*cut)
    return loudness


def cumulative_ranks(amount, slope):
    loads = [(1 << 20) // math.isqrt(rank ** slope) + 1 for rank in range(1, amount + 1)]
    scale = 1 + sum(loads) // (1 << 30)
    return np.cumsum(np.array([max(1, weight // scale) for weight in loads]))


def skewed_ids(stream_key, extent, count, skew):
    table = cumulative_ranks(count, skew)
    pick = jax.random.randint(jax.random.fold_in(stream_key, 1), extent, 0, int(table[count - 1]))
    grade = jnp.searchsorted(jnp.asarray(table, jnp.int32), pick, side="right")
    return jax.random.permutation(jax.random.fold_in(stream_key, 2), count)[grade].astype(jnp.int32)


def gaussian(own_key, extent, deviation, bound, cuts=(), held_as=jnp.bfloat16):
    gain = block_levels(own_key, extent, cuts, -0.22, 0.18) if cuts else 1.0
    entries = jax.random.normal(own_key, extent, jnp.float32) * deviation * gain
    return jnp.minimum(jnp.maximum(entries, -bound), bound).astype(held_as)


def setup_inputs(seed: int = 0) -> dict:
    seeds = jax.random.split(jax.random.key(seed), 12)
    frac = jnp.clip(1.0 * jax.random.uniform(seeds[0], (3, NX, NY, NZ, CAP), jnp.float32) ** block_levels(seeds[0], (3, NX, NY, NZ, CAP), ((1, 4), (2, 2), (3, 4)), -0.2, 0.2), 0.0, 1.0)
    velocity = gaussian(seeds[1], (3, NX, NY, NZ, CAP), 0.3, 2.0, ((1, 4), (2, 2), (3, 4)), jnp.float32)
    force_old = gaussian(seeds[2], (3, NX, NY, NZ, CAP), 1.0, 6.0, ((1, 4), (2, 2), (3, 4)), jnp.float32)
    species = set_ends(skewed_ids(seeds[3], (NX, NY, NZ, CAP), NSPEC, 2), jax.random.fold_in(seeds[3], 3), 0, NSPEC - 1).astype(jnp.int32)
    cell_count = draw_cell_count(jax.random.fold_in(seeds[11], 71), 0)
    neighbours = draw_neighbours(jax.random.fold_in(seeds[11], 71), 0)
    embed = gaussian(seeds[6], (NSPEC, CH), 1.0, 6.0)
    w_radial_in = gaussian(seeds[7], (NB, CH), NB ** -0.5, 2.0)
    w_radial_out = gaussian(seeds[8], (CH, 3 * CH), CH ** -0.5, 0.75)
    w_node = gaussian(seeds[9], (4 * CH, CH), (4 * CH) ** -0.5, 0.375)
    w_energy = gaussian(seeds[10], (CH,), CH ** -0.5, 0.75, (), jnp.float32)
    return {"frac": frac, "velocity": velocity, "force_old": force_old, "species": species, "cell_count": cell_count, "neighbours": neighbours, "embed": embed, "w_radial_in": w_radial_in, "w_radial_out": w_radial_out, "w_node": w_node, "w_energy": w_energy}


MASSES = (1.008, 12.011, 14.007, 15.999, 32.06, 22.99, 35.45, 39.098, 24.305, 40.078)
SQRT3 = 1.7320508075688772
HALF_SQRT3 = 0.8660254037844386
TIME_STEP = 0.5

def species_mass(species):
    table = jnp.asarray(MASSES, dtype=jnp.float32) / 16.0
    shape_ones = (1,) * species.ndim
    which = species[None] == jnp.arange(len(MASSES), dtype=jnp.int32).reshape((-1,) + shape_ones)
    return lax.optimization_barrier(jnp.sum(jnp.where(which, table.reshape((-1,) + shape_ones), 0.0), axis=0))

def embed_species(species_flat, embed):
    kinds = embed.shape[0]
    onehot = (species_flat[None, :] == jnp.arange(kinds, dtype=jnp.int32)[:, None]).astype(jnp.bfloat16)
    return jnp.dot(embed.T, onehot, preferred_element_type=jnp.float32).astype(jnp.bfloat16)

def site_terms(displace, send_feat, own_feat, w_radial_in, w_radial_out, w_node, w_energy):
    basis_count = w_radial_in.shape[0]
    channels = own_feat.shape[0]
    candidates = displace.shape[1]
    block_size = displace.shape[2]
    squared = lax.optimization_barrier(jnp.sum(displace * displace, axis=0))
    envelope = jnp.maximum(1.0 - squared, 0.0) ** 3
    centres = jnp.arange(basis_count, dtype=jnp.float32) / (basis_count - 1)
    basis_values = jnp.exp(-float((basis_count - 1) ** 2) * (squared[None] - centres[:, None, None]) ** 2)
    basis_values = basis_values.astype(jnp.bfloat16).reshape(basis_count, candidates * block_size)
    hidden = jax.nn.silu(jnp.dot(w_radial_in.T, basis_values, preferred_element_type=jnp.float32)).astype(jnp.bfloat16)
    radial = jnp.dot(w_radial_out.T, hidden, preferred_element_type=jnp.float32)
    radial = radial.reshape(3, channels, candidates, block_size) * envelope[None, None]
    along_x = displace[0]
    along_y = displace[1]
    along_z = displace[2]
    first_order = jnp.stack([along_x, along_y, along_z])
    second_order = jnp.stack([SQRT3 * along_x * along_y, SQRT3 * along_y * along_z, SQRT3 * along_z * along_x, HALF_SQRT3 * (along_x * along_x - along_y * along_y), 0.5 * (2.0 * along_z * along_z - along_x * along_x - along_y * along_y)])
    carried = radial * send_feat.astype(jnp.float32)[None]
    scalar_part = lax.optimization_barrier(jnp.sum(carried[0], axis=1))
    vector_part = lax.optimization_barrier(jnp.sum(carried[1][None] * first_order[:, None], axis=2))
    tensor_part = lax.optimization_barrier(jnp.sum(carried[2][None] * second_order[:, None], axis=2))
    invariant = jnp.concatenate([scalar_part, lax.optimization_barrier(jnp.sum(vector_part * vector_part, axis=0)), lax.optimization_barrier(jnp.sum(tensor_part * tensor_part, axis=0)), own_feat.astype(jnp.float32)], axis=0).astype(jnp.bfloat16)
    activity = jax.nn.silu(jnp.dot(w_node.T, invariant, preferred_element_type=jnp.float32))
    return lax.optimization_barrier(jnp.sum(w_energy[:, None] * activity, axis=0))

def reference(frac, velocity, force_old, species, cell_count, neighbours, embed, w_radial_in, w_radial_out, w_node, w_energy):
    cells_x, cells_y, cells_z, capacity = species.shape
    candidates = neighbours.shape[0]
    total = cells_x * cells_y * cells_z * capacity
    block_size = 16 * capacity
    occupied = (lax.broadcasted_iota(jnp.int32, species.shape, 3) < cell_count[..., None]).astype(jnp.float32)
    atom_mass = species_mass(species)
    half_velocity = velocity + 0.5 * TIME_STEP * force_old / atom_mass
    moved = frac + TIME_STEP * half_velocity
    feats = embed_species(species.reshape(total), embed)
    moved_flat = moved.reshape(3, total)
    codes = neighbours.reshape(candidates, total)
    occupied_flat = occupied.reshape(total)

    def one_block(carried, number):
        forces, energies = carried
        start = number * block_size
        receivers = start + jnp.arange(block_size, dtype=jnp.int32)
        cell_id = receivers // capacity
        cell_a = cell_id // (cells_y * cells_z)
        cell_b = cell_id // cells_z % cells_y
        cell_c = cell_id % cells_z
        packed = lax.dynamic_slice_in_dim(codes, start, block_size, 1)
        offset = packed // capacity
        slot_id = packed % capacity
        shift_a = offset // 9 - 1
        shift_b = offset // 3 % 3 - 1
        shift_c = offset % 3 - 1
        senders = (((cell_a + shift_a) % cells_x * cells_y + (cell_b + shift_b) % cells_y) * cells_z + (cell_c + shift_c) % cells_z) * capacity + slot_id
        cell_shift = jnp.stack([shift_a, shift_b, shift_c]).astype(jnp.float32)
        own_pos = lax.dynamic_slice_in_dim(moved_flat, start, block_size, 1)
        displace = cell_shift + moved_flat[:, senders] - own_pos[:, None, :]
        send_feat = feats[:, senders]
        own_feat = lax.dynamic_slice_in_dim(feats, start, block_size, 1)
        weights = lax.dynamic_slice_in_dim(occupied_flat, start, block_size, 0)

        def energy_of(shifted):
            return site_terms(shifted, send_feat, own_feat, w_radial_in, w_radial_out, w_node, w_energy)
        energy, pullback = jax.vjp(energy_of, displace)
        gradient = pullback(weights)[0]
        forces = forces.at[:, receivers].add(lax.optimization_barrier(jnp.sum(gradient, axis=1)))
        forces = forces.at[:, senders.reshape(-1)].add(-gradient.reshape(3, -1))
        energies = lax.dynamic_update_slice_in_dim(energies, energy, start, 0)
        return ((forces, energies), None)
    start_state = (jnp.zeros((3, total), jnp.float32), jnp.zeros((total,), jnp.float32))
    blocks = jnp.arange(total // block_size, dtype=jnp.int32)
    (forces, energies), _ = lax.scan(one_block, start_state, blocks)
    next_force = occupied * forces.reshape(3, cells_x, cells_y, cells_z, capacity)
    next_velocity = occupied * (half_velocity + 0.5 * TIME_STEP * next_force / atom_mass)
    next_frac = occupied * moved
    site_energy = occupied * energies.reshape(cells_x, cells_y, cells_z, capacity)
    return (next_frac, next_velocity, next_force, site_energy)
```

```python
import functools
import itertools

import jax
import jax.numpy as jnp
from jax import lax
from jax.experimental import pallas as pl
from jax.experimental.pallas import tpu as pltpu
from jax.sharding import PartitionSpec as P

MASSES = (1.008, 12.011, 14.007, 15.999, 32.06, 22.99, 35.45, 39.098, 24.305, 40.078)
SQRT3 = 1.7320508075688772
HALF_SQRT3 = 0.8660254037844386
TIME_STEP = 0.5
AXES = ("gx", "gy", "gz")
MESH = pl.DeviceIdType.MESH
F32 = jnp.float32
BF16 = jnp.bfloat16
GROUP = 4


def canonical(coordinate, cells, total):
    return coordinate % total if total < cells + 2 else coordinate


def halo_plan(cells, sizes):
    totals = [c * s for c, s in zip(cells, sizes)]
    spans = [sorted({canonical(e, c, t) for e in range(-1, c + 1)}) for c, t in zip(cells, totals)]
    plan = []
    for at in itertools.product(*spans):
        step = tuple(e // c for e, c in zip(at, cells))
        inner = tuple(e % c for e, c in zip(at, cells))
        plan.append((at, step, inner))
    return spans, totals, plan


def dot(a, b, ca=1, cb=0):
    return lax.dot_general(a, b, (((ca,), (cb,)), ((), ())), preferred_element_type=F32)


def silu_parts(pre):
    sig = 0.5 * jnp.tanh(0.5 * pre) + 0.5
    return pre * sig, sig * (1.0 + pre * (1.0 - sig))


def harmonics(x, y, z):
    return (
        None,
        x,
        y,
        z,
        SQRT3 * x * y,
        SQRT3 * y * z,
        SQRT3 * z * x,
        HALF_SQRT3 * (x * x - y * y),
        0.5 * (2.0 * z * z - x * x - y * y),
    )


DEGREE = (0, 1, 1, 1, 2, 2, 2, 2, 2)


def step_kernel(
    sizes,
    frac,
    velocity,
    force_old,
    species,
    cell_count,
    neighbours,
    embed,
    w_in,
    w_out,
    w_node,
    w_energy,
    next_frac,
    next_velocity,
    next_force,
    site_energy,
    table,
    back,
    landed,
    onehot,
    spread,
    prod,
    feat_s,
    slope,
    basis_s,
    ysc,
    gsc,
    rows_s,
    msg,
    send_a,
    recv_a,
    send_b,
    recv_b,
):
    cells = species.shape[:3]
    cap = species.shape[3]
    cand = neighbours.shape[0]
    chan = embed.shape[1]
    kinds = embed.shape[0]
    nb = w_in.shape[0]
    spans, totals, plan = halo_plan(cells, sizes)
    index_of = {at: i for i, (at, _, _) in enumerate(plan)}
    inner_cells = list(itertools.product(*[range(c) for c in cells]))
    me = [lax.axis_index(a) for a in AXES]

    def device(step):
        return {
            a: lax.rem(m + s + n, n) for a, m, s, n in zip(AXES, me, step, sizes)
        }

    moves = [(i, step, inner) for i, (_, step, inner) in enumerate(plan) if any(s % n for s, n in zip(step, sizes))]
    others = sorted({tuple(s % n for s, n in zip(step, sizes)) for _, step, _ in moves})
    barrier = pltpu.get_barrier_semaphore()
    for step in others:
        pl.semaphore_signal(barrier, inc=1, device_id=device(step), device_id_type=MESH)

    rows = {}
    for c, (a, b, z) in enumerate(inner_cells):
        kind = species[a, b, pl.ds(z, 1), :]
        mass = jnp.zeros((1, cap), F32)
        for n, value in enumerate(MASSES):
            mass = jnp.where(kind == n, value / 16.0, mass)
        lane = lax.broadcasted_iota(jnp.int32, (1, cap), 1)
        occ = (lane < cell_count[a, b, z]).astype(F32)
        e = index_of[(a, b, z)]
        moved, half = [], []
        for d in range(3):
            h = velocity[d, a, b, pl.ds(z, 1), :] + 0.5 * TIME_STEP * force_old[d, a, b, pl.ds(z, 1), :] / mass
            m = frac[d, a, b, pl.ds(z, 1), :] + TIME_STEP * h
            table[e, d : d + 1, :] = m
            next_frac[d, a, b, pl.ds(z, 1), :] = occ * m
            half.append(h)
            moved.append(m)
        table[e, 3:4, :] = kind.astype(F32)
        rows[c] = (kind, mass, occ, moved, half)

    shift_bits = cap.bit_length() - 1
    pairs = {}
    slot_rows = lax.broadcasted_iota(jnp.int32, (cap, cap), 0)
    for c, (a, b, z) in enumerate(inner_cells):
        code = neighbours[:, a, b, z, :]
        if cap == 1 << shift_bits:
            offset, slot = code >> shift_bits, code & (cap - 1)
        else:
            offset, slot = code // cap, code % cap
        third = (offset * 43) >> 7
        ninth = (offset * 57) >> 9
        shifts = (ninth - 1, third - 3 * ninth - 1, offset - 3 * third - 1)
        cell = jnp.zeros_like(code)
        for axis in range(3):
            at = (a, b, z)[axis] + shifts[axis]
            low = spans[axis][0]
            if totals[axis] < cells[axis] + 2:
                at = jnp.where(at < 0, at + totals[axis], at)
                at = jnp.where(at >= totals[axis], at - totals[axis], at)
            cell = cell * len(spans[axis]) + (at - low)
        pairs[c] = (slot, cell, [s.astype(F32) for s in shifts])
        for k in range(cand):
            hit = slot_rows == slot[k : k + 1, :]
            onehot[:, pl.ds((c * cand + k) * cap, cap)] = jnp.where(hit, 1.0, 0.0).astype(BF16)

    pl.semaphore_wait(barrier, len(others))
    copies = []
    for i, step, inner in moves:
        copy = pltpu.make_async_remote_copy(
            src_ref=table.at[index_of[inner]],
            dst_ref=table.at[i],
            send_sem=send_a.at[i],
            recv_sem=recv_a.at[i],
            device_id=device(tuple(-s for s in step)),
            device_id_type=MESH,
        )
        copy.start()
        copies.append(copy)

    w_in_t = w_in[...].astype(F32).T.astype(BF16)
    w_out_t = w_out[...].astype(F32).T.astype(BF16)
    w_node_t = w_node[...].astype(F32).T.astype(BF16)
    diag = lax.broadcasted_iota(jnp.int32, (chan, chan), 0) == lax.broadcasted_iota(jnp.int32, (chan, chan), 1)
    energy_row = jnp.broadcast_to(w_energy[...], (chan, chan))
    energy_col = jnp.sum(jnp.where(diag, energy_row, 0.0), axis=1, keepdims=True)
    kind_rows = lax.broadcasted_iota(jnp.int32, (kinds, cap), 0)
    kind_rows_f = kind_rows.astype(F32)
    centres = lax.broadcasted_iota(jnp.int32, (nb, cap), 0).astype(F32) / (nb - 1)
    own_feat = {
        c: dot(embed[...], (kind_rows == rows[c][0]).astype(F32).astype(BF16), 0, 0).astype(BF16)
        for c in rows
    }

    for copy in copies:
        copy.wait_recv()

    geometry = {}
    for c, (a, b, z) in enumerate(inner_cells):
        slot, cell, shifts = pairs[c]
        found = [jnp.zeros((cand, cap), F32) for _ in range(4)]
        near = sorted(
            {
                index_of[tuple(canonical(p + s, n, t) for p, s, n, t in zip((a, b, z), move, cells, totals))]
                for move in itertools.product((-1, 0, 1), repeat=3)
            }
        )
        for e in near:
            hit = cell == e
            for q in range(4):
                row = jnp.broadcast_to(table[e, q : q + 1, :], (cand, cap))
                found[q] = jnp.where(hit, jnp.take_along_axis(row, slot, axis=1), found[q])
        x, y, w = [s + f - m for s, f, m in zip(shifts, found, rows[c][3])]
        squared = x * x + y * y + w * w
        rest = jnp.maximum(1.0 - squared, 0.0)
        envelope = rest * rest * rest
        geometry[c] = (x, y, w, squared, rest, envelope)
        at = pl.ds(c * cand, cand)
        rows_s[0, at, :] = squared
        rows_s[1, at, :] = found[3]
        for m, value in enumerate(harmonics(x, y, w)):
            ysc[m, at, :] = envelope if value is None else value * envelope

    groups = cand // GROUP
    for c, (a, b, z) in enumerate(inner_cells):
        occ = rows[c][2]
        msg[...] = jnp.zeros_like(msg)

        def forward(g, carry):
            first = c * cand + g * GROUP
            lanes = pl.ds(pl.multiple_of(first * cap, GROUP * cap), GROUP * cap)
            basis, hot = [], []
            for k in range(GROUP):
                gap = rows_s[0, pl.ds(first + k, 1), :] - centres
                basis.append(jnp.exp(-float((nb - 1) ** 2) * (gap * gap)))
                hot.append(jnp.where(kind_rows_f == rows_s[1, pl.ds(first + k, 1), :], 1.0, 0.0))
            basis = jnp.concatenate(basis, axis=1)
            hot = jnp.concatenate(hot, axis=1).astype(BF16)
            basis_s[:, lanes] = basis
            hidden, tilt = silu_parts(dot(w_in_t, basis.astype(BF16)))
            slope[:, lanes] = tilt
            radial = dot(w_out_t, hidden.astype(BF16))
            feat = dot(embed[...], hot, 0, 0)
            feat_s[:, lanes] = feat
            carried = [radial[d * chan : (d + 1) * chan] * feat for d in range(3)]
            for d in range(3):
                prod[d * chan : (d + 1) * chan, lanes] = carried[d]
            for m in range(9):
                total = msg[m]
                for k in range(GROUP):
                    weight = ysc[m, pl.ds(first + k, 1), :]
                    total = total + carried[DEGREE[m]][:, k * cap : (k + 1) * cap] * weight
                msg[m] = total
            return carry

        lax.fori_loop(0, groups, forward, 0)

        vector = msg[1] * msg[1] + msg[2] * msg[2] + msg[3] * msg[3]
        tensor = msg[4] * msg[4]
        for m in range(5, 9):
            tensor = tensor + msg[m] * msg[m]
        invariant = jnp.concatenate([msg[0].astype(BF16), vector.astype(BF16), tensor.astype(BF16), own_feat[c]], axis=0)
        active, tilt = silu_parts(dot(w_node_t, invariant))
        site_energy[a, b, pl.ds(z, 1), :] = occ * jnp.sum(energy_col * active, axis=0, keepdims=True)
        d_pre = (energy_col * occ * tilt).astype(BF16)
        d_inv = dot(w_node[0 : 3 * chan, :], d_pre).astype(BF16).astype(F32)
        msg[0] = d_inv[0:chan]
        for m in range(1, 9):
            part = d_inv[DEGREE[m] * chan : (DEGREE[m] + 1) * chan]
            msg[m] = 2.0 * msg[m] * part

        def backward(g, carry):
            first = c * cand + g * GROUP
            lanes = pl.ds(pl.multiple_of(first * cap, GROUP * cap), GROUP * cap)
            d_radial = []
            for k in range(GROUP):
                part = pl.ds(pl.multiple_of((first + k) * cap, cap), cap)
                sums = [None, None, None]
                for m in range(9):
                    d = DEGREE[m]
                    grad = msg[m]
                    gsc[m, pl.ds(first + k, 1), :] = jnp.sum(
                        prod[d * chan : (d + 1) * chan, part] * grad, axis=0, keepdims=True
                    )
                    term = grad * ysc[m, pl.ds(first + k, 1), :]
                    sums[d] = term if sums[d] is None else sums[d] + term
                feat = feat_s[:, part]
                d_radial.append(jnp.concatenate([(s * feat).astype(BF16) for s in sums], axis=0))
            d_radial = jnp.concatenate(d_radial, axis=1)
            d_hidden = dot(w_out[...], d_radial).astype(BF16).astype(F32)
            d_pre_h = (d_hidden * slope[:, lanes]).astype(BF16)
            d_basis = dot(w_in[...], d_pre_h).astype(BF16).astype(F32) * basis_s[:, lanes]
            for k in range(GROUP):
                gap = rows_s[0, pl.ds(first + k, 1), :] - centres
                piece = d_basis[:, k * cap : (k + 1) * cap] * gap
                rows_s[2, pl.ds(first + k, 1), :] = -2.0 * float((nb - 1) ** 2) * jnp.sum(
                    piece, axis=0, keepdims=True
                )
            return carry

        lax.fori_loop(0, groups, backward, 0)

    forces = {}
    quads = spread.shape[0] // 8
    sub = lax.broadcasted_iota(jnp.int32, (8, cap), 0)
    upper = (sub >= 4).astype(jnp.int32)
    for c, (a, b, z) in enumerate(inner_cells):
        x, y, w, squared, rest, envelope = geometry[c]
        at = pl.ds(c * cand, cand)
        grads = [gsc[m, at, :] for m in range(9)]
        d_env = grads[0]
        for m, value in enumerate(harmonics(x, y, w)):
            if m:
                d_env = d_env + value * grads[m]
        d_sq = 2.0 * (rows_s[2, at, :] - 3.0 * rest * rest * d_env)
        h = [None] + [envelope * grads[m] for m in range(1, 9)]
        gx = x * d_sq + h[1] + SQRT3 * (y * h[4] + w * h[6] + x * h[7]) - x * h[8]
        gy = y * d_sq + h[2] + SQRT3 * (x * h[4] + w * h[5] - y * h[7]) - y * h[8]
        gz = w * d_sq + h[3] + SQRT3 * (y * h[5] + x * h[6]) + 2.0 * w * h[8]
        gradient = (gx, gy, gz)
        forces[c] = [jnp.sum(g, axis=0, keepdims=True) for g in gradient]
        cell = pairs[c][1]
        for k in range(cand):
            block = jnp.zeros((8, cap), F32)
            for d in range(3):
                block = jnp.where((sub & 3) == d, -gradient[d][k : k + 1, :], block)
            where = cell[k : k + 1, :] - upper
            lanes = pl.ds((c * cand + k) * cap, cap)
            pieces = [jnp.where(where == 2 * q, block, 0.0) for q in range(quads)]
            spread[:, lanes] = jnp.concatenate(pieces, axis=0).astype(BF16)

    scattered = dot(spread[...], onehot[...], 1, 1)
    for i in range(len(plan)):
        back[i] = scattered[4 * i : 4 * i + 4]
    returns = []
    for i, step, inner in moves:
        copy = pltpu.make_async_remote_copy(
            src_ref=back.at[i],
            dst_ref=landed.at[i],
            send_sem=send_b.at[i],
            recv_sem=recv_b.at[i],
            device_id=device(step),
            device_id_type=MESH,
        )
        copy.start()
        returns.append(copy)
    for copy in copies:
        copy.wait_send()
    for copy in returns:
        copy.wait_recv()
    remote = {i for i, _, _ in moves}
    for c, (a, b, z) in enumerate(inner_cells):
        kind, mass, occ, moved, half = rows[c]
        total = jnp.zeros((4, cap), F32)
        for i, (_, _, inner) in enumerate(plan):
            if inner == (a, b, z):
                total = total + (landed[i] if i in remote else back[i])
        for d in range(3):
            force = occ * (forces[c][d] + total[d : d + 1])
            next_force[d, a, b, pl.ds(z, 1), :] = force
            next_velocity[d, a, b, pl.ds(z, 1), :] = occ * (half[d] + 0.5 * TIME_STEP * force / mass)
    for copy in returns:
        copy.wait_send()


def solution(mesh):
    sizes = tuple(mesh.shape[a] for a in AXES)

    def shards(frac, velocity, force_old, species, cell_count, neighbours, embed, w_in, w_out, w_node, w_energy):
        cells, cap = species.shape[:3], species.shape[3]
        cand, chan, nb = neighbours.shape[0], embed.shape[1], w_in.shape[0]
        _, _, plan = halo_plan(cells, sizes)
        count = cells[0] * cells[1] * cells[2]
        pair_rows = count * cand
        wide = pair_rows * cap
        held = len(plan)
        spread_rows = -(-4 * held // 16) * 16
        vmem = pl.BlockSpec(memory_space=pltpu.VMEM)
        smem = pl.BlockSpec(memory_space=pltpu.SMEM)
        field = jax.ShapeDtypeStruct(frac.shape, F32)
        return pl.pallas_call(
            functools.partial(step_kernel, sizes),
            out_shape=(field, field, field, jax.ShapeDtypeStruct(species.shape, F32)),
            in_specs=[vmem] * 4 + [smem] + [vmem] * 6,
            out_specs=(vmem,) * 4,
            scratch_shapes=[
                pltpu.VMEM((held, 4, cap), F32),
                pltpu.VMEM((held, 4, cap), F32),
                pltpu.VMEM((held, 4, cap), F32),
                pltpu.VMEM((cap, wide), BF16),
                pltpu.VMEM((spread_rows, wide), BF16),
                pltpu.VMEM((3 * chan, wide), F32),
                pltpu.VMEM((chan, wide), F32),
                pltpu.VMEM((chan, wide), F32),
                pltpu.VMEM((nb, wide), F32),
                pltpu.VMEM((9, pair_rows, cap), F32),
                pltpu.VMEM((9, pair_rows, cap), F32),
                pltpu.VMEM((3, pair_rows, cap), F32),
                pltpu.VMEM((9, chan, cap), F32),
                pltpu.SemaphoreType.DMA((held,)),
                pltpu.SemaphoreType.DMA((held,)),
                pltpu.SemaphoreType.DMA((held,)),
                pltpu.SemaphoreType.DMA((held,)),
            ],
            compiler_params=pltpu.CompilerParams(collective_id=0, has_side_effects=True),
        )(frac, velocity, force_old, species, cell_count, neighbours, embed, w_in, w_out, w_node, w_energy.reshape(1, -1))

    field = P(None, "gx", "gy", "gz", None)
    cell = P("gx", "gy", "gz", None)
    return jax.shard_map(
        shards,
        mesh=mesh,
        in_specs=(field, field, field, cell, P("gx", "gy", "gz"), field, P(), P(), P(), P(), P()),
        out_specs=(field, field, field, cell),
        check_vma=False,
    )
```

```python
import functools
import itertools

import jax
import jax.numpy as jnp
from jax import lax
from jax.experimental import pallas as pl
from jax.experimental.pallas import tpu as pltpu
from jax.sharding import PartitionSpec as P

MASSES = (1.008, 12.011, 14.007, 15.999, 32.06, 22.99, 35.45, 39.098, 24.305, 40.078)
SQRT3 = 1.7320508075688772
HALF_SQRT3 = 0.8660254037844386
TIME_STEP = 0.5
AXES = ("gx", "gy", "gz")
MESH = pl.DeviceIdType.MESH
F32 = jnp.float32
BF16 = jnp.bfloat16
GROUP = 16
INPUTS = 11


def canonical(coordinate, cells, total):
    return coordinate % total if total < cells + 2 else coordinate


def halo_plan(cells, sizes):
    totals = [c * s for c, s in zip(cells, sizes)]
    spans = [sorted({canonical(e, c, t) for e in range(-1, c + 1)}) for c, t in zip(cells, totals)]
    plan = []
    for at in itertools.product(*spans):
        step = tuple(e // c for e, c in zip(at, cells))
        inner = tuple(e % c for e, c in zip(at, cells))
        plan.append((at, step, inner))
    return spans, totals, plan


def dot(a, b, ca=1, cb=0):
    return lax.dot_general(a, b, (((ca,), (cb,)), ((), ())), preferred_element_type=F32)


def silu_parts(pre):
    sig = 0.5 * jnp.tanh(0.5 * pre) + 0.5
    return pre * sig, sig * (1.0 + pre * (1.0 - sig))


def harmonics(x, y, z):
    return (
        None,
        x,
        y,
        z,
        SQRT3 * x * y,
        SQRT3 * y * z,
        SQRT3 * z * x,
        HALF_SQRT3 * (x * x - y * y),
        0.5 * (2.0 * z * z - x * x - y * y),
    )


DEGREE = (0, 1, 1, 1, 2, 2, 2, 2, 2)


def step_kernel(sizes, *refs):
    sources, outs, held = refs[:INPUTS], refs[INPUTS : INPUTS + 4], refs[INPUTS + 4 :]
    next_frac, next_velocity, next_force, site_energy = outs
    staged, held = held[:INPUTS], held[INPUTS:]
    frac, velocity, force_old, species, cell_count, neighbours, embed, w_in, w_out, w_node_t, w_energy = staged
    (table, back, landed, onehot, spread, prod, feat_s, slope, basis_s, ysc, gsc, rows_s, msg) = held[:13]
    send_a, recv_a, send_b, recv_b, load_sem = held[13:]
    loads = [pltpu.make_async_copy(sources[i], staged[i], load_sem.at[i]) for i in range(INPUTS)]
    for load in loads:
        load.start()
    cells = species.shape[:3]
    cap = species.shape[3]
    cand = neighbours.shape[0]
    chan = embed.shape[1]
    kinds = embed.shape[0]
    nb = w_in.shape[0]
    spans, totals, plan = halo_plan(cells, sizes)
    index_of = {at: i for i, (at, _, _) in enumerate(plan)}
    inner_cells = list(itertools.product(*[range(c) for c in cells]))
    me = [lax.axis_index(a) for a in AXES]

    def device(step):
        return {
            a: lax.rem(m + s + n, n) for a, m, s, n in zip(AXES, me, step, sizes)
        }

    moves = [(i, step, inner) for i, (_, step, inner) in enumerate(plan) if any(s % n for s, n in zip(step, sizes))]
    others = sorted({tuple(s % n for s, n in zip(step, sizes)) for _, step, _ in moves})
    barrier = pltpu.get_barrier_semaphore()
    for step in others:
        pl.semaphore_signal(barrier, inc=1, device_id=device(step), device_id_type=MESH)

    for load in loads[:6]:
        load.wait()

    rows = {}
    for c, (a, b, z) in enumerate(inner_cells):
        kind = species[a, b, pl.ds(z, 1), :]
        mass = jnp.zeros((1, cap), F32)
        for n, value in enumerate(MASSES):
            mass = jnp.where(kind == n, value / 16.0, mass)
        lane = lax.broadcasted_iota(jnp.int32, (1, cap), 1)
        occ = (lane < cell_count[a, b, z]).astype(F32)
        e = index_of[(a, b, z)]
        moved, half = [], []
        for d in range(3):
            h = velocity[d, a, b, pl.ds(z, 1), :] + 0.5 * TIME_STEP * force_old[d, a, b, pl.ds(z, 1), :] / mass
            m = frac[d, a, b, pl.ds(z, 1), :] + TIME_STEP * h
            table[e, d : d + 1, :] = m
            next_frac[d, a, b, pl.ds(z, 1), :] = occ * m
            half.append(h)
            moved.append(m)
        table[e, 3:4, :] = kind.astype(F32)
        rows[c] = (kind, mass, occ, moved, half)

    shift_bits = cap.bit_length() - 1
    pairs = {}
    slot_rows = lax.broadcasted_iota(jnp.int32, (cap, cap), 0)
    for c, (a, b, z) in enumerate(inner_cells):
        code = neighbours[:, a, b, z, :]
        if cap == 1 << shift_bits:
            offset, slot = code >> shift_bits, code & (cap - 1)
        else:
            offset, slot = code // cap, code % cap
        third = (offset * 43) >> 7
        ninth = (offset * 57) >> 9
        shifts = (ninth - 1, third - 3 * ninth - 1, offset - 3 * third - 1)
        cell = jnp.zeros_like(code)
        for axis in range(3):
            at = (a, b, z)[axis] + shifts[axis]
            low = spans[axis][0]
            if totals[axis] < cells[axis] + 2:
                at = jnp.where(at < 0, at + totals[axis], at)
                at = jnp.where(at >= totals[axis], at - totals[axis], at)
            cell = cell * len(spans[axis]) + (at - low)
        pairs[c] = (slot, cell, [s.astype(F32) for s in shifts])
        for k in range(cand):
            hit = slot_rows == slot[k : k + 1, :]
            onehot[:, pl.ds((c * cand + k) * cap, cap)] = jnp.where(hit, 1.0, 0.0).astype(BF16)

    pl.semaphore_wait(barrier, len(others))
    copies = []
    for i, step, inner in moves:
        copy = pltpu.make_async_remote_copy(
            src_ref=table.at[index_of[inner]],
            dst_ref=table.at[i],
            send_sem=send_a.at[i],
            recv_sem=recv_a.at[i],
            device_id=device(tuple(-s for s in step)),
            device_id_type=MESH,
        )
        copy.start()
        copies.append(copy)

    for load in loads[6:]:
        load.wait()
    w_in_t = w_in[...].astype(F32).T.astype(BF16)
    w_out_t = w_out[...].astype(F32).T.astype(BF16)
    diag = lax.broadcasted_iota(jnp.int32, (chan, chan), 0) == lax.broadcasted_iota(jnp.int32, (chan, chan), 1)
    energy_row = jnp.broadcast_to(w_energy[...], (chan, chan))
    energy_col = jnp.sum(jnp.where(diag, energy_row, 0.0), axis=1, keepdims=True)
    kind_rows = lax.broadcasted_iota(jnp.int32, (kinds, cap), 0)
    kind_rows_f = kind_rows.astype(F32)
    centres = lax.broadcasted_iota(jnp.int32, (nb, cap), 0).astype(F32) / (nb - 1)
    own_feat = {
        c: dot(embed[...], (kind_rows == rows[c][0]).astype(F32).astype(BF16), 0, 0).astype(BF16)
        for c in rows
    }

    for copy in copies:
        copy.wait_recv()

    geometry = {}
    for c, (a, b, z) in enumerate(inner_cells):
        slot, cell, shifts = pairs[c]
        found = [jnp.zeros((cand, cap), F32) for _ in range(4)]
        near = sorted(
            {
                index_of[tuple(canonical(p + s, n, t) for p, s, n, t in zip((a, b, z), move, cells, totals))]
                for move in itertools.product((-1, 0, 1), repeat=3)
            }
        )
        for e in near:
            hit = cell == e
            for q in range(4):
                row = jnp.broadcast_to(table[e, q : q + 1, :], (cand, cap))
                found[q] = jnp.where(hit, jnp.take_along_axis(row, slot, axis=1), found[q])
        x, y, w = [s + f - m for s, f, m in zip(shifts, found, rows[c][3])]
        squared = x * x + y * y + w * w
        rest = jnp.maximum(1.0 - squared, 0.0)
        envelope = rest * rest * rest
        geometry[c] = (x, y, w, squared, rest, envelope)
        at = pl.ds(c * cand, cand)
        rows_s[0, at, :] = squared
        rows_s[1, at, :] = found[3]
        for m, value in enumerate(harmonics(x, y, w)):
            ysc[m, at, :] = envelope if value is None else value * envelope

    groups = cand // GROUP
    for c, (a, b, z) in enumerate(inner_cells):
        occ = rows[c][2]
        msg[...] = jnp.zeros_like(msg)

        def forward(g, carry):
            first = c * cand + g * GROUP
            lanes = pl.ds(pl.multiple_of(first * cap, GROUP * cap), GROUP * cap)
            basis, hot = [], []
            for k in range(GROUP):
                gap = rows_s[0, pl.ds(first + k, 1), :] - centres
                basis.append(jnp.exp(-float((nb - 1) ** 2) * (gap * gap)))
                hot.append(jnp.where(kind_rows_f == rows_s[1, pl.ds(first + k, 1), :], 1.0, 0.0))
            basis = jnp.concatenate(basis, axis=1)
            hot = jnp.concatenate(hot, axis=1).astype(BF16)
            basis_s[:, lanes] = basis
            hidden, tilt = silu_parts(dot(w_in_t, basis.astype(BF16)))
            slope[:, lanes] = tilt
            radial = dot(w_out_t, hidden.astype(BF16))
            feat = dot(embed[...], hot, 0, 0)
            feat_s[:, lanes] = feat
            carried = [radial[d * chan : (d + 1) * chan] * feat for d in range(3)]
            for d in range(3):
                prod[d * chan : (d + 1) * chan, lanes] = carried[d]
            for m in range(9):
                total = msg[m]
                for k in range(GROUP):
                    weight = ysc[m, pl.ds(first + k, 1), :]
                    total = total + carried[DEGREE[m]][:, k * cap : (k + 1) * cap] * weight
                msg[m] = total
            return carry

        lax.fori_loop(0, groups, forward, 0)

        vector = msg[1] * msg[1] + msg[2] * msg[2] + msg[3] * msg[3]
        tensor = msg[4] * msg[4]
        for m in range(5, 9):
            tensor = tensor + msg[m] * msg[m]
        invariant = jnp.concatenate([msg[0].astype(BF16), vector.astype(BF16), tensor.astype(BF16), own_feat[c]], axis=0)
        active, tilt = silu_parts(dot(w_node_t[...], invariant))
        site_energy[a, b, pl.ds(z, 1), :] = occ * jnp.sum(energy_col * active, axis=0, keepdims=True)
        d_pre = (energy_col * occ * tilt).astype(BF16)
        d_inv = dot(w_node_t[:, 0 : 3 * chan], d_pre, 0, 0).astype(BF16).astype(F32)
        msg[0] = d_inv[0:chan]
        for m in range(1, 9):
            part = d_inv[DEGREE[m] * chan : (DEGREE[m] + 1) * chan]
            msg[m] = 2.0 * msg[m] * part

        def backward(g, carry):
            first = c * cand + g * GROUP
            lanes = pl.ds(pl.multiple_of(first * cap, GROUP * cap), GROUP * cap)
            d_radial = []
            for k in range(GROUP):
                part = pl.ds(pl.multiple_of((first + k) * cap, cap), cap)
                sums = [None, None, None]
                for m in range(9):
                    d = DEGREE[m]
                    grad = msg[m]
                    gsc[m, pl.ds(first + k, 1), :] = jnp.sum(
                        prod[d * chan : (d + 1) * chan, part] * grad, axis=0, keepdims=True
                    )
                    term = grad * ysc[m, pl.ds(first + k, 1), :]
                    sums[d] = term if sums[d] is None else sums[d] + term
                feat = feat_s[:, part]
                d_radial.append(jnp.concatenate([(s * feat).astype(BF16) for s in sums], axis=0))
            d_radial = jnp.concatenate(d_radial, axis=1)
            d_hidden = dot(w_out[...], d_radial).astype(BF16).astype(F32)
            d_pre_h = (d_hidden * slope[:, lanes]).astype(BF16)
            d_basis = dot(w_in[...], d_pre_h).astype(BF16).astype(F32) * basis_s[:, lanes]
            for k in range(GROUP):
                gap = rows_s[0, pl.ds(first + k, 1), :] - centres
                piece = d_basis[:, k * cap : (k + 1) * cap] * gap
                rows_s[2, pl.ds(first + k, 1), :] = -2.0 * float((nb - 1) ** 2) * jnp.sum(
                    piece, axis=0, keepdims=True
                )
            return carry

        lax.fori_loop(0, groups, backward, 0)

    forces = {}
    quads = spread.shape[0] // 8
    sub = lax.broadcasted_iota(jnp.int32, (8, cap), 0)
    upper = (sub >= 4).astype(jnp.int32)
    for c, (a, b, z) in enumerate(inner_cells):
        x, y, w, squared, rest, envelope = geometry[c]
        at = pl.ds(c * cand, cand)
        grads = [gsc[m, at, :] for m in range(9)]
        d_env = grads[0]
        for m, value in enumerate(harmonics(x, y, w)):
            if m:
                d_env = d_env + value * grads[m]
        d_sq = 2.0 * (rows_s[2, at, :] - 3.0 * rest * rest * d_env)
        h = [None] + [envelope * grads[m] for m in range(1, 9)]
        gx = x * d_sq + h[1] + SQRT3 * (y * h[4] + w * h[6] + x * h[7]) - x * h[8]
        gy = y * d_sq + h[2] + SQRT3 * (x * h[4] + w * h[5] - y * h[7]) - y * h[8]
        gz = w * d_sq + h[3] + SQRT3 * (y * h[5] + x * h[6]) + 2.0 * w * h[8]
        gradient = (gx, gy, gz)
        forces[c] = [jnp.sum(g, axis=0, keepdims=True) for g in gradient]
        cell = pairs[c][1]
        for k in range(cand):
            block = jnp.zeros((8, cap), F32)
            for d in range(3):
                block = jnp.where((sub & 3) == d, -gradient[d][k : k + 1, :], block)
            where = cell[k : k + 1, :] - upper
            lanes = pl.ds((c * cand + k) * cap, cap)
            pieces = [jnp.where(where == 2 * q, block, 0.0) for q in range(quads)]
            spread[:, lanes] = jnp.concatenate(pieces, axis=0).astype(BF16)

    scattered = dot(spread[...], onehot[...], 1, 1)
    for i in range(len(plan)):
        back[i] = scattered[4 * i : 4 * i + 4]
    returns = []
    for i, step, inner in moves:
        copy = pltpu.make_async_remote_copy(
            src_ref=back.at[i],
            dst_ref=landed.at[i],
            send_sem=send_b.at[i],
            recv_sem=recv_b.at[i],
            device_id=device(step),
            device_id_type=MESH,
        )
        copy.start()
        returns.append(copy)
    for copy in copies:
        copy.wait_send()
    for copy in returns:
        copy.wait_recv()
    remote = {i for i, _, _ in moves}
    for c, (a, b, z) in enumerate(inner_cells):
        kind, mass, occ, moved, half = rows[c]
        total = jnp.zeros((4, cap), F32)
        for i, (_, _, inner) in enumerate(plan):
            if inner == (a, b, z):
                total = total + (landed[i] if i in remote else back[i])
        for d in range(3):
            force = occ * (forces[c][d] + total[d : d + 1])
            next_force[d, a, b, pl.ds(z, 1), :] = force
            next_velocity[d, a, b, pl.ds(z, 1), :] = occ * (half[d] + 0.5 * TIME_STEP * force / mass)
    for copy in returns:
        copy.wait_send()


def hand_over(*refs):
    half = len(refs) // 2
    for source, target in zip(refs[:half], refs[half:]):
        target[...] = source[...]


def solution(mesh):
    sizes = tuple(mesh.shape[a] for a in AXES)

    def shards(frac, velocity, force_old, species, cell_count, neighbours, embed, w_in, w_out, w_node, w_energy):
        cells, cap = species.shape[:3], species.shape[3]
        cand, chan, nb = neighbours.shape[0], embed.shape[1], w_in.shape[0]
        _, _, plan = halo_plan(cells, sizes)
        count = cells[0] * cells[1] * cells[2]
        pair_rows = count * cand
        wide = pair_rows * cap
        held = len(plan)
        spread_rows = -(-4 * held // 16) * 16
        vmem = pl.BlockSpec(memory_space=pltpu.VMEM)
        operands = (frac, velocity, force_old, species, cell_count, neighbours)
        operands += (embed, w_in, w_out, w_node.T, w_energy.reshape(1, -1))
        staged = [pltpu.VMEM(o.shape, o.dtype) for o in operands]
        staged[4] = pltpu.SMEM(cell_count.shape, cell_count.dtype)
        field = jax.ShapeDtypeStruct(frac.shape, F32)
        results = (field, field, field, jax.ShapeDtypeStruct(species.shape, F32))
        outs = pl.pallas_call(
            functools.partial(step_kernel, sizes),
            out_shape=results,
            in_specs=[pl.BlockSpec(memory_space=pl.ANY)] * INPUTS,
            out_specs=(vmem,) * 4,
            scratch_shapes=staged
            + [
                pltpu.VMEM((held, 4, cap), F32),
                pltpu.VMEM((held, 4, cap), F32),
                pltpu.VMEM((held, 4, cap), F32),
                pltpu.VMEM((cap, wide), BF16),
                pltpu.VMEM((spread_rows, wide), BF16),
                pltpu.VMEM((3 * chan, wide), F32),
                pltpu.VMEM((chan, wide), F32),
                pltpu.VMEM((chan, wide), F32),
                pltpu.VMEM((nb, wide), F32),
                pltpu.VMEM((9, pair_rows, cap), F32),
                pltpu.VMEM((9, pair_rows, cap), F32),
                pltpu.VMEM((3, pair_rows, cap), F32),
                pltpu.VMEM((9, chan, cap), F32),
                pltpu.SemaphoreType.DMA((held,)),
                pltpu.SemaphoreType.DMA((held,)),
                pltpu.SemaphoreType.DMA((held,)),
                pltpu.SemaphoreType.DMA((held,)),
                pltpu.SemaphoreType.DMA((INPUTS,)),
            ],
            compiler_params=pltpu.CompilerParams(collective_id=0, has_side_effects=True),
        )(*operands)
        return pl.pallas_call(hand_over, out_shape=results, in_specs=[vmem] * 4, out_specs=(vmem,) * 4)(*outs)

    field = P(None, "gx", "gy", "gz", None)
    cell = P("gx", "gy", "gz", None)
    return jax.shard_map(
        shards,
        mesh=mesh,
        in_specs=(field, field, field, cell, P("gx", "gy", "gz"), field, P(), P(), P(), P(), P()),
        out_specs=(field, field, field, cell),
        check_vma=False,
    )
```

```python
import functools
import itertools

import jax
import jax.numpy as jnp
from jax import lax
from jax.experimental import pallas as pl
from jax.experimental.pallas import tpu as pltpu
from jax.sharding import PartitionSpec as P

MASSES = (1.008, 12.011, 14.007, 15.999, 32.06, 22.99, 35.45, 39.098, 24.305, 40.078)
SQRT3 = 1.7320508075688772
HALF_SQRT3 = 0.8660254037844386
TIME_STEP = 0.5
AXES = ("gx", "gy", "gz")
MESH = pl.DeviceIdType.MESH
F32 = jnp.float32
BF16 = jnp.bfloat16
GROUP = 16
INPUTS = 11


def canonical(coordinate, cells, total):
    return coordinate % total if total < cells + 2 else coordinate


def halo_plan(cells, sizes):
    totals = [c * s for c, s in zip(cells, sizes)]
    spans = [sorted({canonical(e, c, t) for e in range(-1, c + 1)}) for c, t in zip(cells, totals)]
    plan = []
    for at in itertools.product(*spans):
        step = tuple(e // c for e, c in zip(at, cells))
        inner = tuple(e % c for e, c in zip(at, cells))
        plan.append((at, step, inner))
    return spans, totals, plan


def dot(a, b, ca=1, cb=0):
    return lax.dot_general(a, b, (((ca,), (cb,)), ((), ())), preferred_element_type=F32)


def repeat(count, body):
    if count == 1:
        body(0, 0)
    else:
        lax.fori_loop(0, count, body, 0)


def aligned(start, unit):
    return start if isinstance(start, int) else pl.multiple_of(start, unit)


def silu_parts(pre):
    sig = 0.5 * jnp.tanh(0.5 * pre) + 0.5
    return pre * sig, sig * (1.0 + pre * (1.0 - sig))


def harmonics(x, y, z):
    return (
        None,
        x,
        y,
        z,
        SQRT3 * x * y,
        SQRT3 * y * z,
        SQRT3 * z * x,
        HALF_SQRT3 * (x * x - y * y),
        0.5 * (2.0 * z * z - x * x - y * y),
    )


DEGREE = (0, 1, 1, 1, 2, 2, 2, 2, 2)


def step_kernel(sizes, *refs):
    sources, outs, held = refs[:INPUTS], refs[INPUTS : INPUTS + 4], refs[INPUTS + 4 :]
    next_frac, next_velocity, next_force, site_energy = outs
    staged, held = held[:INPUTS], held[INPUTS:]
    frac, velocity, force_old, species, cell_count, neighbours, embed, w_in, w_out, w_node_t, w_energy = staged
    (table, back, landed, onehot, spread, prod, feat_s, slope, basis_s, ysc, gsc, rows_s, msg) = held[:13]
    send_a, recv_a, send_b, recv_b, load_sem = held[13:]
    sums_of = msg
    loads = [pltpu.make_async_copy(sources[i], staged[i], load_sem.at[i]) for i in range(INPUTS)]
    for load in loads:
        load.start()
    cells = species.shape[:3]
    cap = species.shape[3]
    cand = neighbours.shape[0]
    chan = embed.shape[1]
    kinds = embed.shape[0]
    nb = w_in.shape[0]
    spans, totals, plan = halo_plan(cells, sizes)
    index_of = {at: i for i, (at, _, _) in enumerate(plan)}
    inner_cells = list(itertools.product(*[range(c) for c in cells]))
    me = [lax.axis_index(a) for a in AXES]

    def device(step):
        return {
            a: lax.rem(m + s + n, n) for a, m, s, n in zip(AXES, me, step, sizes)
        }

    moves = [(i, step, inner) for i, (_, step, inner) in enumerate(plan) if any(s % n for s, n in zip(step, sizes))]
    others = sorted({tuple(s % n for s, n in zip(step, sizes)) for _, step, _ in moves})
    barrier = pltpu.get_barrier_semaphore()
    for step in others:
        pl.semaphore_signal(barrier, inc=1, device_id=device(step), device_id_type=MESH)

    for load in loads[:6]:
        load.wait()

    rows = {}
    for c, (a, b, z) in enumerate(inner_cells):
        kind = species[a, b, pl.ds(z, 1), :]
        mass = jnp.zeros((1, cap), F32)
        for n, value in enumerate(MASSES):
            mass = jnp.where(kind == n, value / 16.0, mass)
        lane = lax.broadcasted_iota(jnp.int32, (1, cap), 1)
        occ = (lane < cell_count[a, b, z]).astype(F32)
        e = index_of[(a, b, z)]
        moved, half = [], []
        for d in range(3):
            h = velocity[d, a, b, pl.ds(z, 1), :] + 0.5 * TIME_STEP * force_old[d, a, b, pl.ds(z, 1), :] / mass
            m = frac[d, a, b, pl.ds(z, 1), :] + TIME_STEP * h
            table[e, d : d + 1, :] = m
            next_frac[d, a, b, pl.ds(z, 1), :] = occ * m
            half.append(h)
            moved.append(m)
        table[e, 3:4, :] = kind.astype(F32)
        rows[c] = (kind, mass, occ, moved, half)

    shift_bits = cap.bit_length() - 1
    pairs = {}
    slot_rows = lax.broadcasted_iota(jnp.int32, (cap, cap), 0)
    for c, (a, b, z) in enumerate(inner_cells):
        code = neighbours[:, a, b, z, :]
        if cap == 1 << shift_bits:
            offset, slot = code >> shift_bits, code & (cap - 1)
        else:
            offset, slot = code // cap, code % cap
        third = (offset * 43) >> 7
        ninth = (offset * 57) >> 9
        shifts = (ninth - 1, third - 3 * ninth - 1, offset - 3 * third - 1)
        cell = jnp.zeros_like(code)
        for axis in range(3):
            at = (a, b, z)[axis] + shifts[axis]
            low = spans[axis][0]
            if totals[axis] < cells[axis] + 2:
                at = jnp.where(at < 0, at + totals[axis], at)
                at = jnp.where(at >= totals[axis], at - totals[axis], at)
            cell = cell * len(spans[axis]) + (at - low)
        pairs[c] = (slot, cell, [s.astype(F32) for s in shifts])
        for k in range(cand):
            hit = slot_rows == slot[k : k + 1, :]
            onehot[:, pl.ds((c * cand + k) * cap, cap)] = jnp.where(hit, 1.0, 0.0).astype(BF16)

    pl.semaphore_wait(barrier, len(others))
    copies = []
    for i, step, inner in moves:
        copy = pltpu.make_async_remote_copy(
            src_ref=table.at[index_of[inner]],
            dst_ref=table.at[i],
            send_sem=send_a.at[i],
            recv_sem=recv_a.at[i],
            device_id=device(tuple(-s for s in step)),
            device_id_type=MESH,
        )
        copy.start()
        copies.append(copy)

    for load in loads[6:]:
        load.wait()
    w_in_t = w_in[...].astype(F32).T.astype(BF16)
    w_out_t = w_out[...].astype(F32).T.astype(BF16)
    diag = lax.broadcasted_iota(jnp.int32, (chan, chan), 0) == lax.broadcasted_iota(jnp.int32, (chan, chan), 1)
    energy_row = jnp.broadcast_to(w_energy[...], (chan, chan))
    energy_col = jnp.sum(jnp.where(diag, energy_row, 0.0), axis=1, keepdims=True)
    kind_rows = lax.broadcasted_iota(jnp.int32, (kinds, cap), 0)
    kind_rows_f = kind_rows.astype(F32)
    centres = lax.broadcasted_iota(jnp.int32, (nb, cap), 0).astype(F32) / (nb - 1)
    own_feat = {
        c: dot(embed[...], (kind_rows == rows[c][0]).astype(F32).astype(BF16), 0, 0).astype(BF16)
        for c in rows
    }

    for copy in copies:
        copy.wait_recv()

    geometry = {}
    for c, (a, b, z) in enumerate(inner_cells):
        slot, cell, shifts = pairs[c]
        found = [jnp.zeros((cand, cap), F32) for _ in range(4)]
        near = sorted(
            {
                index_of[tuple(canonical(p + s, n, t) for p, s, n, t in zip((a, b, z), move, cells, totals))]
                for move in itertools.product((-1, 0, 1), repeat=3)
            }
        )
        for e in near:
            hit = cell == e
            for q in range(4):
                row = jnp.broadcast_to(table[e, q : q + 1, :], (cand, cap))
                found[q] = jnp.where(hit, jnp.take_along_axis(row, slot, axis=1), found[q])
        x, y, w = [s + f - m for s, f, m in zip(shifts, found, rows[c][3])]
        squared = x * x + y * y + w * w
        rest = jnp.maximum(1.0 - squared, 0.0)
        envelope = rest * rest * rest
        geometry[c] = (x, y, w, squared, rest, envelope)
        at = pl.ds(c * cand, cand)
        rows_s[0, at, :] = squared
        rows_s[1, at, :] = found[3]
        for m, value in enumerate(harmonics(x, y, w)):
            ysc[m, at, :] = envelope if value is None else value * envelope

    groups = cand // GROUP
    for c, (a, b, z) in enumerate(inner_cells):
        msg = sums_of.at[c]
        msg[...] = jnp.zeros((9, chan, cap), F32)

        def forward(g, carry, c=c, msg=msg):
            first = c * cand + g * GROUP
            lanes = pl.ds(aligned(first * cap, GROUP * cap), GROUP * cap)
            basis, hot = [], []
            for k in range(GROUP):
                gap = rows_s[0, pl.ds(first + k, 1), :] - centres
                basis.append(jnp.exp(-float((nb - 1) ** 2) * (gap * gap)))
                hot.append(jnp.where(kind_rows_f == rows_s[1, pl.ds(first + k, 1), :], 1.0, 0.0))
            basis = jnp.concatenate(basis, axis=1)
            hot = jnp.concatenate(hot, axis=1).astype(BF16)
            basis_s[:, lanes] = basis
            hidden, tilt = silu_parts(dot(w_in_t, basis.astype(BF16)))
            slope[:, lanes] = tilt
            radial = dot(w_out_t, hidden.astype(BF16))
            feat = dot(embed[...], hot, 0, 0)
            feat_s[:, lanes] = feat
            carried = [radial[d * chan : (d + 1) * chan] * feat for d in range(3)]
            for d in range(3):
                prod[d * chan : (d + 1) * chan, lanes] = carried[d]
            for m in range(9):
                total = msg[m]
                for k in range(GROUP):
                    weight = ysc[m, pl.ds(first + k, 1), :]
                    total = total + carried[DEGREE[m]][:, k * cap : (k + 1) * cap] * weight
                msg[m] = total
            return carry

        repeat(groups, forward)

    for c, (a, b, z) in enumerate(inner_cells):
        occ, msg = rows[c][2], sums_of.at[c]
        vector = msg[1] * msg[1] + msg[2] * msg[2] + msg[3] * msg[3]
        tensor = msg[4] * msg[4]
        for m in range(5, 9):
            tensor = tensor + msg[m] * msg[m]
        invariant = jnp.concatenate([msg[0].astype(BF16), vector.astype(BF16), tensor.astype(BF16), own_feat[c]], axis=0)
        active, tilt = silu_parts(dot(w_node_t[...], invariant))
        site_energy[a, b, pl.ds(z, 1), :] = occ * jnp.sum(energy_col * active, axis=0, keepdims=True)
        d_pre = (energy_col * occ * tilt).astype(BF16)
        d_inv = dot(w_node_t[:, 0 : 3 * chan], d_pre, 0, 0).astype(BF16).astype(F32)
        msg[0] = d_inv[0:chan]
        for m in range(1, 9):
            part = d_inv[DEGREE[m] * chan : (DEGREE[m] + 1) * chan]
            msg[m] = 2.0 * msg[m] * part

    for c, (a, b, z) in enumerate(inner_cells):
        msg = sums_of.at[c]

        def backward(g, carry, c=c, msg=msg):
            first = c * cand + g * GROUP
            lanes = pl.ds(aligned(first * cap, GROUP * cap), GROUP * cap)
            d_radial = []
            for k in range(GROUP):
                part = pl.ds(aligned((first + k) * cap, cap), cap)
                sums = [None, None, None]
                for m in range(9):
                    d = DEGREE[m]
                    grad = msg[m]
                    gsc[m, pl.ds(first + k, 1), :] = jnp.sum(
                        prod[d * chan : (d + 1) * chan, part] * grad, axis=0, keepdims=True
                    )
                    term = grad * ysc[m, pl.ds(first + k, 1), :]
                    sums[d] = term if sums[d] is None else sums[d] + term
                feat = feat_s[:, part]
                d_radial.append(jnp.concatenate([(s * feat).astype(BF16) for s in sums], axis=0))
            d_radial = jnp.concatenate(d_radial, axis=1)
            d_hidden = dot(w_out[...], d_radial).astype(BF16).astype(F32)
            d_pre_h = (d_hidden * slope[:, lanes]).astype(BF16)
            d_basis = dot(w_in[...], d_pre_h).astype(BF16).astype(F32) * basis_s[:, lanes]
            for k in range(GROUP):
                gap = rows_s[0, pl.ds(first + k, 1), :] - centres
                piece = d_basis[:, k * cap : (k + 1) * cap] * gap
                rows_s[2, pl.ds(first + k, 1), :] = -2.0 * float((nb - 1) ** 2) * jnp.sum(
                    piece, axis=0, keepdims=True
                )
            return carry

        repeat(groups, backward)

    forces = {}
    quads = spread.shape[0] // 8
    sub = lax.broadcasted_iota(jnp.int32, (8, cap), 0)
    upper = (sub >= 4).astype(jnp.int32)
    for c, (a, b, z) in enumerate(inner_cells):
        x, y, w, squared, rest, envelope = geometry[c]
        at = pl.ds(c * cand, cand)
        grads = [gsc[m, at, :] for m in range(9)]
        d_env = grads[0]
        for m, value in enumerate(harmonics(x, y, w)):
            if m:
                d_env = d_env + value * grads[m]
        d_sq = 2.0 * (rows_s[2, at, :] - 3.0 * rest * rest * d_env)
        h = [None] + [envelope * grads[m] for m in range(1, 9)]
        gx = x * d_sq + h[1] + SQRT3 * (y * h[4] + w * h[6] + x * h[7]) - x * h[8]
        gy = y * d_sq + h[2] + SQRT3 * (x * h[4] + w * h[5] - y * h[7]) - y * h[8]
        gz = w * d_sq + h[3] + SQRT3 * (y * h[5] + x * h[6]) + 2.0 * w * h[8]
        gradient = (gx, gy, gz)
        forces[c] = [jnp.sum(g, axis=0, keepdims=True) for g in gradient]
        cell = pairs[c][1]
        for k in range(cand):
            block = jnp.zeros((8, cap), F32)
            for d in range(3):
                block = jnp.where((sub & 3) == d, -gradient[d][k : k + 1, :], block)
            where = cell[k : k + 1, :] - upper
            lanes = pl.ds((c * cand + k) * cap, cap)
            pieces = [jnp.where(where == 2 * q, block, 0.0) for q in range(quads)]
            spread[:, lanes] = jnp.concatenate(pieces, axis=0).astype(BF16)

    scattered = dot(spread[...], onehot[...], 1, 1)
    for i in range(len(plan)):
        back[i] = scattered[4 * i : 4 * i + 4]
    returns = []
    for i, step, inner in moves:
        copy = pltpu.make_async_remote_copy(
            src_ref=back.at[i],
            dst_ref=landed.at[i],
            send_sem=send_b.at[i],
            recv_sem=recv_b.at[i],
            device_id=device(step),
            device_id_type=MESH,
        )
        copy.start()
        returns.append(copy)
    for copy in copies:
        copy.wait_send()
    for copy in returns:
        copy.wait_recv()
    remote = {i for i, _, _ in moves}
    for c, (a, b, z) in enumerate(inner_cells):
        kind, mass, occ, moved, half = rows[c]
        total = jnp.zeros((4, cap), F32)
        for i, (_, _, inner) in enumerate(plan):
            if inner == (a, b, z):
                total = total + (landed[i] if i in remote else back[i])
        for d in range(3):
            force = occ * (forces[c][d] + total[d : d + 1])
            next_force[d, a, b, pl.ds(z, 1), :] = force
            next_velocity[d, a, b, pl.ds(z, 1), :] = occ * (half[d] + 0.5 * TIME_STEP * force / mass)
    for copy in returns:
        copy.wait_send()


def hand_over(*refs):
    half = len(refs) // 2
    for source, target in zip(refs[:half], refs[half:]):
        target[...] = source[...]


def solution(mesh):
    sizes = tuple(mesh.shape[a] for a in AXES)

    def shards(frac, velocity, force_old, species, cell_count, neighbours, embed, w_in, w_out, w_node, w_energy):
        cells, cap = species.shape[:3], species.shape[3]
        cand, chan, nb = neighbours.shape[0], embed.shape[1], w_in.shape[0]
        _, _, plan = halo_plan(cells, sizes)
        count = cells[0] * cells[1] * cells[2]
        pair_rows = count * cand
        wide = pair_rows * cap
        held = len(plan)
        spread_rows = -(-4 * held // 16) * 16
        vmem = pl.BlockSpec(memory_space=pltpu.VMEM)
        operands = (frac, velocity, force_old, species, cell_count, neighbours)
        operands += (embed, w_in, w_out, w_node.T, w_energy.reshape(1, -1))
        staged = [pltpu.VMEM(o.shape, o.dtype) for o in operands]
        staged[4] = pltpu.SMEM(cell_count.shape, cell_count.dtype)
        field = jax.ShapeDtypeStruct(frac.shape, F32)
        results = (field, field, field, jax.ShapeDtypeStruct(species.shape, F32))
        outs = pl.pallas_call(
            functools.partial(step_kernel, sizes),
            out_shape=results,
            in_specs=[pl.BlockSpec(memory_space=pl.ANY)] * INPUTS,
            out_specs=(vmem,) * 4,
            scratch_shapes=staged
            + [
                pltpu.VMEM((held, 4, cap), F32),
                pltpu.VMEM((held, 4, cap), F32),
                pltpu.VMEM((held, 4, cap), F32),
                pltpu.VMEM((cap, wide), BF16),
                pltpu.VMEM((spread_rows, wide), BF16),
                pltpu.VMEM((3 * chan, wide), F32),
                pltpu.VMEM((chan, wide), F32),
                pltpu.VMEM((chan, wide), F32),
                pltpu.VMEM((nb, wide), F32),
                pltpu.VMEM((9, pair_rows, cap), F32),
                pltpu.VMEM((9, pair_rows, cap), F32),
                pltpu.VMEM((3, pair_rows, cap), F32),
                pltpu.VMEM((count, 9, chan, cap), F32),
                pltpu.SemaphoreType.DMA((held,)),
                pltpu.SemaphoreType.DMA((held,)),
                pltpu.SemaphoreType.DMA((held,)),
                pltpu.SemaphoreType.DMA((held,)),
                pltpu.SemaphoreType.DMA((INPUTS,)),
            ],
            compiler_params=pltpu.CompilerParams(collective_id=0, has_side_effects=True),
        )(*operands)
        return pl.pallas_call(hand_over, out_shape=results, in_specs=[vmem] * 4, out_specs=(vmem,) * 4)(*outs)

    field = P(None, "gx", "gy", "gz", None)
    cell = P("gx", "gy", "gz", None)
    return jax.shard_map(
        shards,
        mesh=mesh,
        in_specs=(field, field, field, cell, P("gx", "gy", "gz"), field, P(), P(), P(), P(), P()),
        out_specs=(field, field, field, cell),
        check_vma=False,
    )
```
